256 devices in a mesh: chan: 8 (over y, core), ctx: 32 (over x, z).
Axes of the slice: x: 4, y: 4, z: 8, core: 2. Of those that a mesh axis runs over, the one named last changes fastest.
Arguments:
- x_one: bfloat16 [4096, 4096], P('ctx', 'chan'), may hold values from -6 to 6
- x_two: bfloat16 [4096, 4096], P('ctx', 'chan'), may hold values from -6 to 6
- values: bfloat16 [4096, 4096], P('ctx', 'chan'), may hold values from -6 to 6
- grad_out: bfloat16 [4096, 4096], P('ctx', 'chan'), may hold values from -6 to 6
- filter_spectrum: float32 [2, 2, 32, 128, 4096], P(None, None, 'ctx', None, 'chan'), may hold values from -6 to 6
- skip_gain: float32 [4096], P('chan'), may hold values from -4 to 4
Outputs:
- d_one: bfloat16 [4096, 4096], P('ctx', 'chan')
- d_two: bfloat16 [4096, 4096], P('ctx', 'chan')
- d_values: bfloat16 [4096, 4096], P('ctx', 'chan')
- d_filter: float32 [2, 2, 32, 128, 4096], P(None, None, 'ctx', None, 'chan')
- d_skip: float32 [4096], P('chan')
The draws below stay inside these ranges and needn't reach their ends.
All inputs are finite; a program needn't handle non-finite values.
Results may differ from the reference program's by a relative error of at most 0.0011.
Values sent between devices are 32-bit elements; how exact they have to be, the bound alone decides.
No kernel may reach another device: no remote copies, remote signals or barrier semaphores. Data moves between devices by JAX's collectives and lax.ppermute only.
A program may use at most 64 MiB of HBM per device.

```python
import jax
import jax.numpy as jnp
import numpy as np

CH = 4096
LOC = 128
SEQ = 4096
N_CTX = 32


def levels(stream_key, dims, split, least, largest):
    loudness, own = 1.0, jax.random.fold_in(stream_key, 6)
    for dim, blocks in split:
        heights = jnp.exp(jax.random.uniform(jax.random.fold_in(own, dim), (blocks,), jnp.float32, least / len(split), largest / len(split)))
        loudness = loudness * jnp.repeat(heights, dims[dim] // blocks).reshape([-1 if axis == dim else 1 for axis in range(len(dims))])
    return loudness


def gaussian(rng, dims, deviation, bound, shards=(), held_as=jnp.bfloat16):
    drawn = deviation * jax.random.normal(rng, dims, jnp.float32)
    if shards:
        drawn = drawn * levels(rng, dims, shards, -0.22, 0.18)
    return jnp.clip(drawn, -bound, bound).astype(held_as)


def setup_inputs(seed: int = 0) -> dict:
    key_list = jax.random.split(jax.random.key(seed), 7)
    return {
        "x_one": gaussian(key_list[0], (SEQ, CH), 1.0, 6.0, ((0, 32), (1, 8))),
        "x_two": gaussian(key_list[1], (SEQ, CH), 1.0, 6.0, ((0, 32), (1, 8))),
        "values": gaussian(key_list[2], (SEQ, CH), 1.0, 6.0, ((0, 32), (1, 8))),
        "grad_out": gaussian(key_list[3], (SEQ, CH), 1.0, 6.0, ((0, 32), (1, 8))),
        "filter_spectrum": gaussian(key_list[4], (2, 2, N_CTX, LOC, CH), 1.0, 6.0, ((2, 32), (4, 8)), jnp.float32),
        "skip_gain": gaussian(key_list[5], (CH,), 1.0, 4.0, ((0, 8),), jnp.float32),
    }


def reversed_order(total_count):
    digits = total_count.bit_length() - 1
    order_list = []
    for position in range(total_count):
        flipped = 0
        for bit_place in range(digits):
            flipped = flipped | (((position >> bit_place) & 1) << (digits - 1 - bit_place))
        order_list.append(flipped)
    return np.array(order_list)


def reference(x_one, x_two, values, grad_out, filter_spectrum, skip_gain):
    grad_prod = grad_out.astype(jnp.float32) * x_two.astype(jnp.float32)
    signal = x_one.astype(jnp.float32) * values.astype(jnp.float32)
    double_len = 2 * SEQ
    rev_table = reversed_order(N_CTX)
    freqs = np.arange(double_len)
    parity = freqs % 2
    halves = freqs // 2
    row_pick = rev_table[halves % N_CTX]
    col_pick = halves // N_CTX
    spec_real = filter_spectrum[0][parity, row_pick, col_pick]
    spec_imag = filter_spectrum[1][parity, row_pick, col_pick]
    spectrum = spec_real + 1j * spec_imag
    grad_freq = jnp.fft.fft(grad_prod, n=double_len, axis=0)
    sig_freq = jnp.fft.fft(signal, n=double_len, axis=0)
    conv = jnp.real(jnp.fft.ifft(spectrum * sig_freq, axis=0))[:SEQ]
    back = jnp.real(jnp.fft.ifft(jnp.conj(spectrum) * grad_freq, axis=0))[:SEQ]
    d_signal = back + skip_gain[None, :] * grad_prod
    d_one = (d_signal * values.astype(jnp.float32)).astype(jnp.bfloat16)
    d_values = (d_signal * x_one.astype(jnp.float32)).astype(jnp.bfloat16)
    d_two = (grad_out.astype(jnp.float32) * (conv + skip_gain[None, :] * signal)).astype(jnp.bfloat16)
    d_spec = jnp.conj(sig_freq) * grad_freq / double_len
    d_spec = jnp.stack([jnp.real(d_spec), jnp.imag(d_spec)])
    d_spec = d_spec.reshape(2, LOC, N_CTX, 2, CH).transpose(0, 3, 2, 1, 4)
    d_filter = d_spec[:, :, rev_table]
    d_skip = jnp.sum(grad_prod * signal, axis=0)
    return d_one, d_two, d_values, d_filter, d_skip
```

```python
import jax
import jax.numpy as jnp
import numpy as np
from jax import lax
from jax.experimental import pallas as pl
from jax.experimental.pallas import tpu as pltpu
from jax.sharding import PartitionSpec as P

N_DEV = 32
LOC = 128
N_FFT = 2 * N_DEV * LOC
CPD = 16
ROWS = 6 * CPD
CB = 128


def split_np(m):
    hi = np.asarray(m, np.float32).astype(jnp.bfloat16)
    lo = (np.asarray(m, np.float64) - hi.astype(np.float64)).astype(np.float32).astype(jnp.bfloat16)
    return hi, lo


def tables():
    rev = np.array([int(format(r, "05b")[::-1], 2) for r in range(N_DEV)])
    q = np.concatenate([2 * rev, 2 * rev + 1])
    d = np.arange(N_DEV)
    m = np.arange(LOC)
    ang = 2 * np.pi * (np.outer(q, d) % 64) / 64.0
    w1 = np.concatenate([np.cos(ang), -np.sin(ang)], axis=0)
    hi, lo = split_np(w1)
    w1c = np.concatenate([hi, hi, lo], axis=1)
    w2 = np.concatenate([np.cos(ang).T, -np.sin(ang).T], axis=1) / N_FFT
    hi, lo = split_np(w2)
    w2c = np.concatenate([hi, hi, lo], axis=1)
    tw = 2 * np.pi * np.outer(q, m) / N_FFT
    tc = np.tile(np.cos(tw), (1, 2)).astype(np.float32)
    ts = np.tile(np.sin(tw), (1, 2)).astype(np.float32)
    bm = 2 * np.pi * (np.outer(m, m) % LOC) / LOC
    c, s = np.cos(bm), np.sin(bm)
    fwd = np.concatenate([np.concatenate([c, -s], 1), np.concatenate([s, c], 1)], 0)
    inv = np.concatenate([np.concatenate([c, s], 1), np.concatenate([-s, c], 1)], 0)
    return (w1c, w2c, tc, ts, *split_np(fwd), *split_np(inv))


def split(v):
    hi = v.astype(jnp.bfloat16)
    lo = (v - hi.astype(jnp.float32)).astype(jnp.bfloat16)
    return hi, lo


def dot(a, b):
    return jnp.dot(a, b, preferred_element_type=jnp.float32)


def pre_kernel(x1, x2, v, go, f, out, ds):
    g = go[...].astype(jnp.float32) * x2[...].astype(jnp.float32)
    z = x1[...].astype(jnp.float32) * v[...].astype(jnp.float32)
    ds[...] = jnp.sum(g * z, axis=0, keepdims=True)
    n = CB // CPD
    out[:, 0:CPD, :] = g.T.reshape(n, CPD, LOC)
    out[:, CPD : 2 * CPD, :] = z.T.reshape(n, CPD, LOC)
    for k in range(4):
        o = (2 + k) * CPD
        out[:, o : o + CPD, :] = f[k // 2, k % 2, 0].T.reshape(n, CPD, LOC)


def rows_of(ref, row):
    return ref[pl.ds(row, N_DEV, stride=ROWS), :]


def mid_kernel(r, w1, w2, tc, ts, fh, fl, ih, il, s, bh, bl, fs):
    def put(row, val):
        s[pl.ds(row, N_DEV, stride=ROWS), :] = val

    def stage(row, val):
        hi, lo = split(val)
        bh[row : row + 64, :] = hi
        bl[row : row + 64, :] = lo

    def big(mh, ml):
        a = bh[...]
        fs[...] = dot(a, mh[...]) + dot(bl[...], mh[...]) + dot(a, ml[...])

    for c in range(CPD):
        x = jnp.concatenate([rows_of(r, c), rows_of(r, CPD + c)], axis=1)
        hi, lo = split(x)
        a = dot(w1[...], jnp.concatenate([hi, lo, hi], axis=0))
        re, im = a[:64], a[64:]
        bre = re * tc[...] + im * ts[...]
        bim = im * tc[...] - re * ts[...]
        stage(c * 128, jnp.concatenate([bre[:, :LOC], bim[:, :LOC]], axis=1))
        stage(c * 128 + 64, jnp.concatenate([bre[:, LOC:], bim[:, LOC:]], axis=1))
    big(fh, fl)
    for c in range(CPD):
        gre = fs[c * 128 : c * 128 + 64, :LOC]
        gim = fs[c * 128 : c * 128 + 64, LOC:]
        zre = fs[c * 128 + 64 : c * 128 + 128, :LOC]
        zim = fs[c * 128 + 64 : c * 128 + 128, LOC:]
        hre = jnp.concatenate([rows_of(r, 2 * CPD + c), rows_of(r, 3 * CPD + c)], axis=0)
        him = jnp.concatenate([rows_of(r, 4 * CPD + c), rows_of(r, 5 * CPD + c)], axis=0)
        dre = (zre * gre + zim * gim) * (1.0 / N_FFT)
        dim = (zre * gim - zim * gre) * (1.0 / N_FFT)
        put(2 * CPD + c, dre[:32])
        put(3 * CPD + c, dre[32:])
        put(4 * CPD + c, dim[:32])
        put(5 * CPD + c, dim[32:])
        stage(c * 128, jnp.concatenate([hre * gre + him * gim, hre * gim - him * gre], axis=1))
        stage(c * 128 + 64, jnp.concatenate([hre * zre - him * zim, hre * zim + him * zre], axis=1))
    big(ih, il)
    for c in range(CPD):
        a = fs[c * 128 : c * 128 + 64, :]
        b = fs[c * 128 + 64 : c * 128 + 128, :]
        re = jnp.concatenate([a[:, :LOC], b[:, :LOC]], axis=1)
        im = jnp.concatenate([a[:, LOC:], b[:, LOC:]], axis=1)
        ure = re * tc[...] - im * ts[...]
        uim = im * tc[...] + re * ts[...]
        hi, lo = split(jnp.concatenate([ure, uim], axis=0))
        o = dot(w2[...], jnp.concatenate([hi, lo, hi], axis=0))
        put(c, o[:, :LOC])
        put(CPD + c, o[:, LOC:])


def post_kernel(r, x1, x2, v, go, sg, d1, d2, dv, df):
    def back(k):
        return r[:, k * CPD : (k + 1) * CPD, :].reshape(CB, LOC).T

    f32 = jnp.float32
    x1f, x2f, vf, gof = (t[...].astype(f32) for t in (x1, x2, v, go))
    gain = sg[...]
    dz = back(0) + gain * (gof * x2f)
    d1[...] = (dz * vf).astype(jnp.bfloat16)
    dv[...] = (dz * x1f).astype(jnp.bfloat16)
    d2[...] = (gof * (back(1) + gain * (x1f * vf))).astype(jnp.bfloat16)
    for k in range(4):
        df[k // 2, k % 2, 0] = back(2 + k)


def per_device(x_one, x_two, values, grad_out, filter_spectrum, skip_gain):
    ch = x_one.shape[1]
    f32 = jnp.float32
    steps = ch // CB
    tab = [jnp.asarray(t) for t in tables()]
    row_spec = pl.BlockSpec((LOC, CB), lambda i: (0, i))
    filt_spec = pl.BlockSpec((2, 2, 1, LOC, CB), lambda i: (0, 0, 0, 0, i))
    pack_spec = pl.BlockSpec((CB // CPD, ROWS, LOC), lambda i: (i, 0, 0))
    vec_spec = pl.BlockSpec((1, CB), lambda i: (0, i))
    packed = jax.ShapeDtypeStruct((N_DEV, ROWS, LOC), f32)
    send, part = pl.pallas_call(
        pre_kernel,
        grid=(steps,),
        in_specs=[row_spec] * 4 + [filt_spec],
        out_specs=[pack_spec, vec_spec],
        out_shape=[packed, jax.ShapeDtypeStruct((1, ch), f32)],
        name="pre",
    )(x_one, x_two, values, grad_out, filter_spectrum)
    d_skip = lax.psum(part[0], "ctx")
    recv = lax.all_to_all(send, "ctx", 0, 0, tiled=True)
    sent = pl.pallas_call(
        mid_kernel,
        out_shape=jax.ShapeDtypeStruct((N_DEV * ROWS, LOC), f32),
        scratch_shapes=[
            pltpu.VMEM((CPD * 128, 256), jnp.bfloat16),
            pltpu.VMEM((CPD * 128, 256), jnp.bfloat16),
            pltpu.VMEM((CPD * 128, 256), f32),
        ],
        name="mid",
    )(recv.reshape(N_DEV * ROWS, LOC), *tab)
    out = lax.all_to_all(sent.reshape(N_DEV, ROWS, LOC), "ctx", 0, 0, tiled=True)
    act = jax.ShapeDtypeStruct((LOC, ch), jnp.bfloat16)
    d_one, d_two, d_values, d_filter = pl.pallas_call(
        post_kernel,
        grid=(steps,),
        in_specs=[pack_spec] + [row_spec] * 4 + [vec_spec],
        out_specs=[row_spec] * 3 + [filt_spec],
        out_shape=[act, act, act, jax.ShapeDtypeStruct(filter_spectrum.shape, f32)],
        name="post",
    )(out, x_one, x_two, values, grad_out, skip_gain[None, :])
    return d_one, d_two, d_values, d_filter, d_skip


def solution(mesh):
    act = P("ctx", "chan")
    filt = P(None, None, "ctx", None, "chan")
    return jax.shard_map(
        per_device,
        mesh=mesh,
        in_specs=(act, act, act, act, filt, P("chan")),
        out_specs=(act, act, act, filt, P("chan")),
        check_vma=False,
    )
```

```python
import jax
import jax.numpy as jnp
import numpy as np
from jax import lax
from jax.experimental import pallas as pl
from jax.experimental.pallas import tpu as pltpu
from jax.sharding import PartitionSpec as P

N_DEV = 32
LOC = 128
N_FFT = 2 * N_DEV * LOC
CPD = 16
ROWS = 6 * CPD
ROWS_OUT = ROWS + 8
CB = 128


def split_np(m):
    hi = np.asarray(m, np.float32).astype(jnp.bfloat16)
    lo = (np.asarray(m, np.float64) - hi.astype(np.float64)).astype(np.float32).astype(jnp.bfloat16)
    return hi, lo


def tables():
    rev = np.array([int(format(r, "05b")[::-1], 2) for r in range(N_DEV)])
    q = np.concatenate([2 * rev, 2 * rev + 1])
    d = np.arange(N_DEV)
    m = np.arange(LOC)
    ang = 2 * np.pi * (np.outer(q, d) % 64) / 64.0
    w1 = np.concatenate([np.cos(ang), -np.sin(ang)], axis=0)
    hi, lo = split_np(w1)
    w1c = np.concatenate([hi, hi, lo], axis=1)
    w2 = np.concatenate([np.cos(ang).T, -np.sin(ang).T], axis=1) / N_FFT
    hi, lo = split_np(w2)
    w2c = np.concatenate([hi, hi, lo], axis=1)
    tw = 2 * np.pi * np.outer(q, m) / N_FFT
    tc = np.tile(np.cos(tw), (1, 2)).astype(np.float32)
    ts = np.tile(np.sin(tw), (1, 2)).astype(np.float32)
    bm = 2 * np.pi * (np.outer(m, m) % LOC) / LOC
    c, s = np.cos(bm), np.sin(bm)
    fwd = np.concatenate([np.concatenate([c, -s], 1), np.concatenate([s, c], 1)], 0)
    inv = np.concatenate([np.concatenate([c, s], 1), np.concatenate([-s, c], 1)], 0)
    return (w1c, w2c, tc, ts, *split_np(fwd), *split_np(inv))


def split(v):
    hi = v.astype(jnp.bfloat16)
    lo = (v - hi.astype(jnp.float32)).astype(jnp.bfloat16)
    return hi, lo


def dot(a, b):
    return jnp.dot(a, b, preferred_element_type=jnp.float32)


def pre_kernel(x1, x2, v, go, f, out):
    g = go[...].astype(jnp.float32) * x2[...].astype(jnp.float32)
    z = x1[...].astype(jnp.float32) * v[...].astype(jnp.float32)
    n = CB // CPD
    out[:, 0:CPD, :] = g.T.reshape(n, CPD, LOC)
    out[:, CPD : 2 * CPD, :] = z.T.reshape(n, CPD, LOC)
    for k in range(4):
        o = (2 + k) * CPD
        out[:, o : o + CPD, :] = f[k // 2, k % 2, 0].T.reshape(n, CPD, LOC)


def rows_of(ref, row):
    return ref[pl.ds(row, N_DEV, stride=ROWS), :]


def mid_kernel(r, w1, w2, tc, ts, fh, fl, ih, il, s, bh, bl, fs):
    def put(row, val):
        s[pl.ds(row, N_DEV, stride=ROWS_OUT), :] = val

    def stage(row, val):
        hi, lo = split(val)
        bh[row : row + 64, :] = hi
        bl[row : row + 64, :] = lo

    def big(mh, ml):
        a = bh[...]
        fs[...] = dot(a, mh[...]) + dot(bl[...], mh[...]) + dot(a, ml[...])

    sums = []
    for c in range(CPD):
        x = jnp.concatenate([rows_of(r, c), rows_of(r, CPD + c)], axis=1)
        sums.append(jnp.sum(x[:, :LOC] * x[:, LOC:], axis=0, keepdims=True))
        hi, lo = split(x)
        a = dot(w1[...], jnp.concatenate([hi, lo, hi], axis=0))
        re, im = a[:64], a[64:]
        bre = re * tc[...] + im * ts[...]
        bim = im * tc[...] - re * ts[...]
        stage(c * 128, jnp.concatenate([bre[:, :LOC], bim[:, :LOC]], axis=1))
        stage(c * 128 + 64, jnp.concatenate([bre[:, LOC:], bim[:, LOC:]], axis=1))
    tot = jnp.sum(jnp.concatenate(sums, axis=0), axis=1, keepdims=True)
    lane = lax.broadcasted_iota(jnp.int32, (CPD, LOC), 1)
    row = lax.broadcasted_iota(jnp.int32, (CPD, LOC), 0)
    place = lax.axis_index("ctx") % (CB // CPD) * CPD
    mine = jnp.where(lane == place + row, jnp.broadcast_to(tot, (CPD, LOC)), 0.0)
    skip = jnp.broadcast_to(jnp.sum(mine, axis=0, keepdims=True), (8, LOC))
    for d in range(N_DEV):
        s[d * ROWS_OUT + ROWS : d * ROWS_OUT + ROWS + 8, :] = skip
    big(fh, fl)
    for c in range(CPD):
        gre = fs[c * 128 : c * 128 + 64, :LOC]
        gim = fs[c * 128 : c * 128 + 64, LOC:]
        zre = fs[c * 128 + 64 : c * 128 + 128, :LOC]
        zim = fs[c * 128 + 64 : c * 128 + 128, LOC:]
        hre = jnp.concatenate([rows_of(r, 2 * CPD + c), rows_of(r, 3 * CPD + c)], axis=0)
        him = jnp.concatenate([rows_of(r, 4 * CPD + c), rows_of(r, 5 * CPD + c)], axis=0)
        dre = (zre * gre + zim * gim) * (1.0 / N_FFT)
        dim = (zre * gim - zim * gre) * (1.0 / N_FFT)
        put(2 * CPD + c, dre[:32])
        put(3 * CPD + c, dre[32:])
        put(4 * CPD + c, dim[:32])
        put(5 * CPD + c, dim[32:])
        stage(c * 128, jnp.concatenate([hre * gre + him * gim, hre * gim - him * gre], axis=1))
        stage(c * 128 + 64, jnp.concatenate([hre * zre - him * zim, hre * zim + him * zre], axis=1))
    big(ih, il)
    for c in range(CPD):
        a = fs[c * 128 : c * 128 + 64, :]
        b = fs[c * 128 + 64 : c * 128 + 128, :]
        re = jnp.concatenate([a[:, :LOC], b[:, :LOC]], axis=1)
        im = jnp.concatenate([a[:, LOC:], b[:, LOC:]], axis=1)
        ure = re * tc[...] - im * ts[...]
        uim = im * tc[...] + re * ts[...]
        hi, lo = split(jnp.concatenate([ure, uim], axis=0))
        o = dot(w2[...], jnp.concatenate([hi, lo, hi], axis=0))
        put(c, o[:, :LOC])
        put(CPD + c, o[:, LOC:])


def post_kernel(r, x1, x2, v, go, sg, d1, d2, dv, df, ds):
    def back(k):
        return r[:, k * CPD : (k + 1) * CPD, :].reshape(CB, LOC).T

    f32 = jnp.float32
    x1f, x2f, vf, gof = (t[...].astype(f32) for t in (x1, x2, v, go))
    gain = sg[...]
    dz = back(0) + gain * (gof * x2f)
    d1[...] = (dz * vf).astype(jnp.bfloat16)
    dv[...] = (dz * x1f).astype(jnp.bfloat16)
    d2[...] = (gof * (back(1) + gain * (x1f * vf))).astype(jnp.bfloat16)
    for k in range(4):
        df[k // 2, k % 2, 0] = back(2 + k)
    ds[...] = jnp.sum(r[:, ROWS, :], axis=0, keepdims=True)


def per_device(x_one, x_two, values, grad_out, filter_spectrum, skip_gain):
    ch = x_one.shape[1]
    f32 = jnp.float32
    steps = ch // CB
    tab = [jnp.asarray(t) for t in tables()]
    row_spec = pl.BlockSpec((LOC, CB), lambda i: (0, i))
    filt_spec = pl.BlockSpec((2, 2, 1, LOC, CB), lambda i: (0, 0, 0, 0, i))
    pack_spec = pl.BlockSpec((CB // CPD, ROWS, LOC), lambda i: (i, 0, 0))
    vec_spec = pl.BlockSpec((1, CB), lambda i: (0, i))
    packed = jax.ShapeDtypeStruct((N_DEV, ROWS, LOC), f32)
    send = pl.pallas_call(
        pre_kernel,
        grid=(steps,),
        in_specs=[row_spec] * 4 + [filt_spec],
        out_specs=pack_spec,
        out_shape=packed,
        name="pre",
    )(x_one, x_two, values, grad_out, filter_spectrum)
    recv = lax.all_to_all(send, "ctx", 0, 0, tiled=True)
    sent = pl.pallas_call(
        mid_kernel,
        out_shape=jax.ShapeDtypeStruct((N_DEV * ROWS_OUT, LOC), f32),
        scratch_shapes=[
            pltpu.VMEM((CPD * 128, 256), jnp.bfloat16),
            pltpu.VMEM((CPD * 128, 256), jnp.bfloat16),
            pltpu.VMEM((CPD * 128, 256), f32),
        ],
        name="mid",
    )(recv.reshape(N_DEV * ROWS, LOC), *tab)
    out = lax.all_to_all(sent.reshape(N_DEV, ROWS_OUT, LOC), "ctx", 0, 0, tiled=True)
    act = jax.ShapeDtypeStruct((LOC, ch), jnp.bfloat16)
    d_one, d_two, d_values, d_filter, d_skip = pl.pallas_call(
        post_kernel,
        grid=(steps,),
        in_specs=[pl.BlockSpec((CB // CPD, ROWS_OUT, LOC), lambda i: (i, 0, 0))] + [row_spec] * 4 + [vec_spec],
        out_specs=[row_spec] * 3 + [filt_spec, vec_spec],
        out_shape=[act, act, act, jax.ShapeDtypeStruct(filter_spectrum.shape, f32), jax.ShapeDtypeStruct((1, ch), f32)],
        name="post",
    )(out, x_one, x_two, values, grad_out, skip_gain[None, :])
    return d_one, d_two, d_values, d_filter, d_skip[0]


def solution(mesh):
    act = P("ctx", "chan")
    filt = P(None, None, "ctx", None, "chan")
    return jax.shard_map(
        per_device,
        mesh=mesh,
        in_specs=(act, act, act, act, filt, P("chan")),
        out_specs=(act, act, act, filt, P("chan")),
        check_vma=False,
    )
```

```python
import jax
import jax.numpy as jnp
import numpy as np
from jax import lax
from jax.experimental import pallas as pl
from jax.experimental.pallas import tpu as pltpu
from jax.sharding import PartitionSpec as P

N_DEV = 32
LOC = 128
N_FFT = 2 * N_DEV * LOC
CPD = 16
CB = 128


def split_np(m):
    hi = np.asarray(m, np.float32).astype(jnp.bfloat16)
    lo = (np.asarray(m, np.float64) - hi.astype(np.float64)).astype(np.float32).astype(jnp.bfloat16)
    return hi, lo


def tables():
    rev = np.array([int(format(r, "05b")[::-1], 2) for r in range(N_DEV)])
    q = np.concatenate([2 * rev, 2 * rev + 1])
    d = np.arange(N_DEV)
    m = np.arange(LOC)
    ang = 2 * np.pi * (np.outer(q, d) % 64) / 64.0
    w1 = np.concatenate([np.cos(ang), -np.sin(ang)], axis=0)
    hi, lo = split_np(w1)
    w1c = np.concatenate([hi, hi, lo], axis=1)
    w2 = np.concatenate([np.cos(ang).T, -np.sin(ang).T], axis=1) / N_FFT
    hi, lo = split_np(w2)
    w2c = np.concatenate([hi, hi, lo], axis=1)
    tw = 2 * np.pi * np.outer(q, m) / N_FFT
    tc = np.tile(np.cos(tw), (1, 2)).astype(np.float32)
    ts = np.tile(np.sin(tw), (1, 2)).astype(np.float32)
    bm = 2 * np.pi * (np.outer(m, m) % LOC) / LOC
    c, s = np.cos(bm), np.sin(bm)
    fwd = np.concatenate([np.concatenate([c, -s], 1), np.concatenate([s, c], 1)], 0)
    inv = np.concatenate([np.concatenate([c, s], 1), np.concatenate([-s, c], 1)], 0)
    return (w1c, w2c, tc, ts, *split_np(fwd), *split_np(inv))


def split(v):
    hi = v.astype(jnp.bfloat16)
    lo = (v - hi.astype(jnp.float32)).astype(jnp.bfloat16)
    return hi, lo


def dot(a, b):
    return jnp.dot(a, b, preferred_element_type=jnp.float32)


N_Z = 8
N_X = 4


def spot():
    here = lax.axis_index("ctx")
    return here // N_Z, here % N_Z


def pre_kernel(dep, x1, x2, v, go, out):
    g = go[...].astype(jnp.float32) * x2[...].astype(jnp.float32)
    z = x1[...].astype(jnp.float32) * v[...].astype(jnp.float32)
    n = CB // CPD
    out[:, 0:CPD, :] = g.T.reshape(n, CPD, LOC)
    out[:, CPD : 2 * CPD, :] = z.T.reshape(n, CPD, LOC)


def filt_kernel(f, o0, o1, o2, o3, tmp):
    mx, mz = spot()
    for l, out in enumerate((o0, o1, o2, o3)):
        cols = pl.ds(pl.multiple_of((l ^ mx) * CB, CB), CB)
        for k in range(4):
            tmp[k] = f[k // 2, k % 2, 0, :, cols].T
        for k in range(4):
            for zz in range(N_Z):
                out[zz, k * CPD : (k + 1) * CPD, :] = tmp[k, pl.ds(pl.multiple_of((zz ^ mz) * CPD, CPD), CPD), :]


def turn_filt(dep, *refs):
    for k in range(N_Z):
        for l in range(N_X):
            refs[N_X + k][l] = refs[l][k]


def turn_out(dep, *refs):
    for k in range(N_Z):
        for l in range(N_X):
            refs[N_X + k][l * 32 : (l + 1) * 32, :] = refs[l][k * 32 : (k + 1) * 32, :]
            refs[N_X + k][128 + l : 129 + l, :] = refs[l][256:257, :]
        refs[N_X + k][132:136, :] = jnp.zeros((4, LOC), jnp.float32)


def rows_of(ref, row, rows):
    return ref[pl.ds(row, N_DEV, stride=rows), :]


def put(ref, row, rows, val):
    ref[pl.ds(row, N_DEV, stride=rows), :] = val


def stage(bh, bl, row, val):
    hi, lo = split(val)
    bh[row : row + 64, :] = hi
    bl[row : row + 64, :] = lo


def big(bh, bl, mh, ml):
    a = bh[...]
    return dot(a, mh[...]) + dot(bl[...], mh[...]) + dot(a, ml[...])


def fwd_kernel(r, w1, tc, ts, fh, fl, fs, s, sk, bh, bl):
    sums = []
    for c in range(CPD):
        x = jnp.concatenate([rows_of(r, c, 2 * CPD), rows_of(r, CPD + c, 2 * CPD)], axis=1)
        sums.append(jnp.sum(x[:, :LOC] * x[:, LOC:], axis=0, keepdims=True))
        hi, lo = split(x)
        a = dot(w1[...], jnp.concatenate([hi, lo, hi], axis=0))
        re, im = a[:64], a[64:]
        bre = re * tc[...] + im * ts[...]
        bim = im * tc[...] - re * ts[...]
        stage(bh, bl, c * 128, jnp.concatenate([bre[:, :LOC], bim[:, :LOC]], axis=1))
        stage(bh, bl, c * 128 + 64, jnp.concatenate([bre[:, LOC:], bim[:, LOC:]], axis=1))
    tot = jnp.sum(jnp.concatenate(sums, axis=0), axis=1, keepdims=True)
    lane = lax.broadcasted_iota(jnp.int32, (CPD, LOC), 1)
    row = lax.broadcasted_iota(jnp.int32, (CPD, LOC), 0)
    mine = jnp.where(lane == spot()[1] * CPD + row, jnp.broadcast_to(tot, (CPD, LOC)), 0.0)
    sk[...] = jnp.broadcast_to(jnp.sum(mine, axis=0, keepdims=True), (8, LOC))
    fs[...] = big(bh, bl, fh, fl)
    for c in range(CPD):
        gre = fs[c * 128 : c * 128 + 64, :LOC]
        gim = fs[c * 128 : c * 128 + 64, LOC:]
        zre = fs[c * 128 + 64 : c * 128 + 128, :LOC]
        zim = fs[c * 128 + 64 : c * 128 + 128, LOC:]
        dre = (zre * gre + zim * gim) * (1.0 / N_FFT)
        dim = (zre * gim - zim * gre) * (1.0 / N_FFT)
        put(s, c, 4 * CPD, dre[:32])
        put(s, CPD + c, 4 * CPD, dre[32:])
        put(s, 2 * CPD + c, 4 * CPD, dim[:32])
        put(s, 3 * CPD + c, 4 * CPD, dim[32:])


def inv_kernel(*refs):
    fs, (sk, w2, tc, ts, ih, il), srcs = refs[0], refs[1:7], refs[7 : 7 + N_Z]
    outs = refs[7 + N_Z : 7 + N_Z + N_X]
    bh, bl, ys, r, s = refs[7 + N_Z + N_X :]
    mx, mz = spot()
    for k in range(N_Z):
        for l in range(N_X):
            dev = (l ^ mx) * N_Z + (k ^ mz)
            r[pl.ds(pl.multiple_of(dev * 64, 64), 64), :] = srcs[k][l]
    for c in range(CPD):
        gre = fs[c * 128 : c * 128 + 64, :LOC]
        gim = fs[c * 128 : c * 128 + 64, LOC:]
        zre = fs[c * 128 + 64 : c * 128 + 128, :LOC]
        zim = fs[c * 128 + 64 : c * 128 + 128, LOC:]
        hre = jnp.concatenate([rows_of(r, c, 4 * CPD), rows_of(r, CPD + c, 4 * CPD)], axis=0)
        him = jnp.concatenate([rows_of(r, 2 * CPD + c, 4 * CPD), rows_of(r, 3 * CPD + c, 4 * CPD)], axis=0)
        stage(bh, bl, c * 128, jnp.concatenate([hre * gre + him * gim, hre * gim - him * gre], axis=1))
        stage(bh, bl, c * 128 + 64, jnp.concatenate([hre * zre - him * zim, hre * zim + him * zre], axis=1))
    ys[...] = big(bh, bl, ih, il)
    for c in range(CPD):
        a = ys[c * 128 : c * 128 + 64, :]
        b = ys[c * 128 + 64 : c * 128 + 128, :]
        re = jnp.concatenate([a[:, :LOC], b[:, :LOC]], axis=1)
        im = jnp.concatenate([a[:, LOC:], b[:, LOC:]], axis=1)
        ure = re * tc[...] - im * ts[...]
        uim = im * tc[...] + re * ts[...]
        hi, lo = split(jnp.concatenate([ure, uim], axis=0))
        o = dot(w2[...], jnp.concatenate([hi, lo, hi], axis=0))
        put(s, c, 2 * CPD, o[:, :LOC])
        put(s, CPD + c, 2 * CPD, o[:, LOC:])
    for l in range(N_X):
        for k in range(N_Z):
            dev = (l ^ mx) * N_Z + (k ^ mz)
            outs[l][k * 32 : (k + 1) * 32, :] = s[pl.ds(pl.multiple_of(dev * 32, 32), 32), :]
        outs[l][256:264, :] = sk[...]


def post_kernel(*refs):
    srcs, (x1, x2, v, go, sg, d1, d2, dv, ds, tmp) = refs[:N_Z], refs[N_Z:]
    f32 = jnp.float32
    mx, mz = spot()
    for l in range(N_X):
        cols = pl.ds(pl.multiple_of((l ^ mx) * CB, CB), CB)
        skip = srcs[0][128 + l : 129 + l, :]
        for k in range(N_Z):
            if k:
                skip = skip + srcs[k][128 + l : 129 + l, :]
            at = pl.ds(pl.multiple_of((k ^ mz) * CPD, CPD), CPD)
            tmp[0, at, :] = srcs[k][l * 32 : l * 32 + CPD, :]
            tmp[1, at, :] = srcs[k][l * 32 + CPD : (l + 1) * 32, :]
        ds[:, cols] = skip
        x1f, x2f, vf, gof = (t[:, cols].astype(f32) for t in (x1, x2, v, go))
        gain = sg[:, cols]
        dz = tmp[0].T + gain * (gof * x2f)
        d1[:, cols] = (dz * vf).astype(jnp.bfloat16)
        dv[:, cols] = (dz * x1f).astype(jnp.bfloat16)
        d2[:, cols] = (gof * (tmp[1].T + gain * (x1f * vf))).astype(jnp.bfloat16)


def dfilt_kernel(r, df):
    for k in range(4):
        df[k // 2, k % 2, 0] = r[:, k * CPD : (k + 1) * CPD, :].reshape(CB, LOC).T


def per_device(x_one, x_two, values, grad_out, filter_spectrum, skip_gain):
    ch = x_one.shape[1]
    f32 = jnp.float32
    bf16 = jnp.bfloat16
    steps = ch // CB
    w1, w2, tc, ts, fh, fl, ih, il = [jnp.asarray(t) for t in tables()]
    any_ = pl.BlockSpec(memory_space=pl.ANY)
    vmem = pl.BlockSpec(memory_space=pltpu.VMEM)
    row_spec = pl.BlockSpec((LOC, CB), lambda i: (0, i))
    filt_spec = pl.BlockSpec((2, 2, 1, LOC, CB), lambda i: (0, 0, 0, 0, i))

    def shape(*dims):
        return jax.ShapeDtypeStruct(dims, f32)

    def pack_spec(k):
        return pl.BlockSpec((CB // CPD, k * CPD, LOC), lambda i: (i, 0, 0))

    def exchange(v):
        return lax.all_to_all(v.reshape(N_DEV, -1, LOC), "ctx", 0, 0, tiled=True)

    def hops(vs, step, order):
        out = list(vs)
        for k in order:
            out[k] = lax.ppermute(vs[k], "ctx", [(d, d ^ (k * step)) for d in range(N_DEV)])
        return out

    x_order = (2, 1, 3)
    z_order = (4, 3, 5, 2, 6, 1, 7)
    half = pltpu.VMEM((CPD * 128, 256), bf16)
    whole = pltpu.VMEM((CPD * 128, 256), f32)
    hx = pl.pallas_call(
        filt_kernel,
        out_shape=[shape(N_Z, 64, LOC)] * N_X,
        scratch_shapes=[pltpu.VMEM((4, LOC, LOC), f32)],
        name="filt",
    )(filter_spectrum)
    s1 = pl.pallas_call(
        pre_kernel,
        grid=(steps,),
        in_specs=[any_] + [row_spec] * 4,
        out_specs=pack_spec(2),
        out_shape=shape(N_DEV, 2 * CPD, LOC),
        name="pre",
    )(hx[0], x_one, x_two, values, grad_out)
    hx = hops(hx, N_Z, x_order)
    r1 = exchange(s1)
    hz = pl.pallas_call(
        turn_filt,
        in_specs=[any_] + [vmem] * N_X,
        out_shape=[shape(N_X, 64, LOC)] * N_Z,
        name="turn_filt",
    )(s1, *hx)
    hz = hops(hz, 1, z_order)
    fs, s3, sk = pl.pallas_call(
        fwd_kernel,
        out_shape=[shape(CPD * 128, 256), shape(N_DEV * 64, LOC), shape(8, LOC)],
        scratch_shapes=[half, half],
        name="fwd",
    )(r1.reshape(-1, LOC), w1, tc, ts, fh, fl)
    r3 = exchange(s3)
    ox = pl.pallas_call(
        inv_kernel,
        out_shape=[shape(264, LOC)] * N_X,
        scratch_shapes=[
            half,
            half,
            whole,
            pltpu.VMEM((N_DEV * 64, LOC), f32),
            pltpu.VMEM((N_DEV * 32, LOC), f32),
        ],
        name="inv",
    )(fs, sk, w2, tc, ts, ih, il, *hz)
    ox = hops(ox, N_Z, x_order)
    oz = pl.pallas_call(
        turn_out,
        in_specs=[any_] + [vmem] * N_X,
        out_shape=[shape(136, LOC)] * N_Z,
        name="turn_out",
    )(sk, *ox)
    oz = hops(oz, 1, z_order)
    d_filter = pl.pallas_call(
        dfilt_kernel,
        grid=(steps,),
        in_specs=[pack_spec(4)],
        out_specs=filt_spec,
        out_shape=shape(*filter_spectrum.shape),
        name="dfilt",
    )(r3)
    act = jax.ShapeDtypeStruct((LOC, ch), bf16)
    d_one, d_two, d_values, d_skip = pl.pallas_call(
        post_kernel,
        out_shape=[act, act, act, shape(1, ch)],
        scratch_shapes=[pltpu.VMEM((2, LOC, LOC), f32)],
        name="post",
    )(*oz, x_one, x_two, values, grad_out, skip_gain[None, :])
    return d_one, d_two, d_values, d_filter, d_skip[0]


def solution(mesh):
    act = P("ctx", "chan")
    filt = P(None, None, "ctx", None, "chan")

    return jax.shard_map(
        per_device,
        mesh=mesh,
        in_specs=(act, act, act, act, filt, P("chan")),
        out_specs=(act, act, act, filt, P("chan")),
        check_vma=False,
    )
```
